128 devices in a mesh: dom: 16 (over y, z), dir: 8 (over x, core).
Axes of the slice: x: 4, y: 4, z: 4, core: 2. Of those that a mesh axis runs over, the one named last changes fastest.
Arguments:
- unknowns: bfloat16 [512, 8, 1024], P(('dom', 'dir')), may hold values from -6 to 6
- schur_blocks: bfloat16 [512, 1024, 1024], P(('dom', 'dir')), may hold values from -0.1875 to 0.1875
- adjacency: int32 [512, 4], P(('dom', 'dir')), may hold values from 0 to 511, as said below
- row_map: int32 [512, 4, 1024], P(('dom', 'dir')), may hold values from 0 to 1023
- coupling: float32 [512, 4, 1024], P(('dom', 'dir')), may hold values from -1.5 to 1.5
- owner_box: int32 [512, 256, 1], P(('dom', 'dir')), may hold values from 0 to 1023; in each aligned block of 1024 rows (0 to 1023, 1024 to 2047, ..., all dimensions but the last counted through in order) at most 2 rows name the same one
- aggregation: bfloat16 [1024, 256, 1152], P('dom', None, 'dir'), may hold values from -0.1875 to 0.1875
- trans_table: float32 [316, 1152], P(None, 'dir'), may hold values from -1.5 to 1.5
- inter_list: int32 [1024, 16], P('dom'), may hold values from 0 to 1023, as said below
- inter_type: int32 [1024, 16], P('dom'), may hold values from 0 to 315
- near_list: int32 [1024, 4], P(('dom', 'dir')), may hold values from 0 to 63
- near_blocks: bfloat16 [1024, 4, 256, 256], P(('dom', 'dir')), may hold values from -0.375 to 0.375
Outputs:
- response: float32 [512, 8, 1024], P(('dom', 'dir'))
The draws below stay inside these ranges and needn't reach their ends.
Inputs may be any that keep to these rules, and one draw needn't show every extreme that they name: `adjacency`: every neighbour t of subdomain s has t // 32 equal to g - 1, g or g + 1 modulo 16, with g = s // 32, and (t // 4) % 8 = (s // 4) % 8. `owner_box`: among the surface unknowns of one aligned block of 4 subdomains, no box is named more than 2 times. `inter_list`: every source box c of box b has c // 64 equal to b // 64 - 1, b // 64 or b // 64 + 1 modulo 16.
All inputs are finite; a program needn't handle non-finite values.
Results may differ from the reference program's by a relative error of at most 0.0035.
Values may be sent and summed in bfloat16 or wider, within the bound.
No kernel may reach another device: no remote copies, remote signals or barrier semaphores. Data moves between devices by JAX's collectives and lax.ppermute only.
A program may use at most 128 MiB of HBM per device.

```python
import math
import jax
import jax.numpy as jnp
import numpy as np
from jax import lax

SUB_DEV = 4
ROWS_SUB = 1024
SURF_ROWS = 256
EXCITES = 8
ADJ_COUNT = 4
BOX_SLOTS = 256
DIRECTIONS = 1152
LIST_LEN = 16
TRANS_TYPES = 316
NEAR_BLOCKS = 4
BOX_DEV = 8
SUBDOMAINS = 512
BOXES = 1024
BOX_GRP = 64
SLOT_CAP = 2
N_DOM = 16
N_DIR = 8


def draw_adjacency(key, part):
    subdomains = SUB_DEV * N_DOM * N_DIR
    first_key, second_key = jax.random.split(jax.random.fold_in(key, 11))
    shifted = jax.random.randint(first_key, (subdomains, ADJ_COUNT), -1, 2)
    within = jax.random.randint(second_key, (subdomains, ADJ_COUNT), 0, SUB_DEV)
    device = jnp.arange(subdomains, dtype=jnp.int32)[:, None] // SUB_DEV
    dom_of = device // N_DIR
    dir_of = device % N_DIR
    target = (dom_of + shifted + N_DOM) % N_DOM * N_DIR + dir_of
    return (target * SUB_DEV + within).astype(jnp.int32)


def draw_inter_list(key, part):
    group_boxes = BOX_DEV * N_DIR
    box_total = group_boxes * N_DOM
    first_key, second_key = jax.random.split(jax.random.fold_in(key, 23))
    shifted = jax.random.randint(first_key, (box_total, LIST_LEN), -1, 2)
    within = jax.random.randint(second_key, (box_total, LIST_LEN), 0, group_boxes)
    group_of = jnp.arange(box_total, dtype=jnp.int32)[:, None] // group_boxes
    target = (group_of + shifted + N_DOM) % N_DOM
    return (target * group_boxes + within).astype(jnp.int32)


def with_ends(result, rng, low, largest):
    longest = result.shape.index(max(result.shape))
    spots = []
    for shift in (0, 1):
        where = [jax.random.randint(jax.random.fold_in(rng, axis), (), 0, length) for axis, length in enumerate(result.shape)]
        where[longest] = (where[longest] + shift) % result.shape[longest]
        spots.append(tuple(where))
    return result.at[spots[0]].set(low).at[spots[1]].set(largest)


def block_levels(own_key, extent, cuts, smallest, top_value):
    gain, own = 1.0, jax.random.fold_in(own_key, 6)
    for position, shards_of in cuts:
        steps = jnp.exp(jax.random.uniform(jax.random.fold_in(own, position), (shards_of,), jnp.float32, smallest / len(cuts), top_value / len(cuts)))
        gain = gain * jnp.repeat(steps, extent[position] // shards_of).reshape([-1 if axis == position else 1 for axis in range(len(extent))])
    return gain


def deal_out(own_key, own, number, rows, number_of, top, limit, slope):
    sequence = jax.random.permutation(own_key, number_of)
    packed, ordinary = portions_of(number_of, rows * top, limit, slope, True), portions_of(number_of, rows * top, limit, slope, False)
    places = jnp.arange(number_of)

    def named(lengths, offset_by):
        used = int((lengths > 0).sum())
        fixed = max(1, used // 4)
        moved = fixed + (places - fixed + offset_by * (used - fixed)) % max(1, number_of - fixed)
        return jnp.zeros((number_of,), jnp.int32).at[sequence[jnp.where(places < fixed, places, moved)]].set(jnp.asarray(lengths, jnp.int32))

    lengths = jnp.where(number % 4 == 0, named(packed, number // 4), named(ordinary, number - number // 4 - 1))
    mixed = jax.random.permutation(jax.random.fold_in(own, 3), number_of)
    source_of, sink = mixed[0:number_of // 2 * 2:2], mixed[1:number_of // 2 * 2:2]
    room = jnp.minimum(lengths[source_of] - 1, limit - lengths[sink]) // 2
    room = jnp.where((source_of == sequence[0]) | (sink == sequence[0]) | (lengths[sink] == 0), 0, jnp.maximum(room, 0))
    moved = jax.random.randint(jax.random.fold_in(own, 4), (number_of // 2,), 0, 1 << 20) % (room + 1)
    lengths = lengths.at[source_of].add(-moved).at[sink].add(moved)
    labels = jnp.searchsorted(jnp.cumsum(lengths), jnp.arange(rows * top), side="right").astype(jnp.int32)
    table = labels.reshape(top, rows).T
    table = table[jax.random.permutation(jax.random.fold_in(own, 1), rows)]
    offset_by = jax.random.randint(jax.random.fold_in(own, 2), (rows, 1), 0, top)
    return jnp.take_along_axis(table, (jnp.arange(top)[None, :] + offset_by) % top, axis=1)


def portions_of(count, total, limit, skew, full):
    loads = [(1 << 20) // math.isqrt(standing ** skew) + 1 for standing in range(1, count + 1)]
    largest = limit if full else min(limit, max(-(-total // count), total * loads[0] // sum(loads)))
    least = 1 if total - largest >= count - 1 else 0
    holding, rest = [largest] + [least] * (count - 1), total - largest - least * (count - 1)
    while rest > 0:
        free = [i for i in range(1, count) if holding[i] < largest] or [i for i in range(1, count) if holding[i] < limit]
        mass, remaining = sum([loads[i] for i in free]), rest
        for i in free:
            more = min(limit - holding[i], max(1, remaining * loads[i] // mass), rest)
            holding[i] = holding[i] + more
            rest = rest - more
    return np.array(holding)


def gaussian(rng, dims, deviation, reach, pieces=(), held_as=jnp.bfloat16):
    result = jax.random.normal(rng, dims, jnp.float32) * deviation
    if len(pieces) > 0:
        result = block_levels(rng, dims, pieces, -0.22, 0.18) * result
    return jnp.clip(result, min=-reach, max=reach).astype(held_as)


def setup_inputs(seed: int = 0) -> dict:
    seeds = jax.random.split(jax.random.key(seed), 13)
    unknowns = gaussian(seeds[0], (SUBDOMAINS, EXCITES, ROWS_SUB), 1.0, 6.0, ((0, 128),))
    schur_blocks = gaussian(seeds[1], (SUBDOMAINS, ROWS_SUB, ROWS_SUB), ROWS_SUB ** -0.5, 0.1875, ((0, 128),))
    adjacency = draw_adjacency(jax.random.fold_in(seeds[12], 71), 0)
    row_map = with_ends(jax.random.randint(seeds[3], (SUBDOMAINS, ADJ_COUNT, ROWS_SUB), 0, ROWS_SUB), jax.random.fold_in(seeds[3], 1), 0, ROWS_SUB - 1).astype(jnp.int32)
    coupling = gaussian(seeds[4], (SUBDOMAINS, ADJ_COUNT, ROWS_SUB), 0.3, 1.5, ((0, 128),), jnp.float32)
    owner_box_keys = jax.random.split(jax.random.fold_in(seeds[5], 1), SUBDOMAINS * SURF_ROWS // (SUB_DEV * SURF_ROWS))
    owner_box_turns = jax.random.permutation(jax.random.fold_in(seeds[5], 3), SUBDOMAINS * SURF_ROWS // (SUB_DEV * SURF_ROWS))
    owner_box = jax.vmap(lambda own, number: deal_out(jax.random.fold_in(seeds[5], 2), own, number, SUB_DEV * SURF_ROWS, BOXES, 1, SLOT_CAP, 2))(owner_box_keys, owner_box_turns).reshape((SUBDOMAINS, SURF_ROWS, 1))
    aggregation = gaussian(seeds[6], (BOXES, BOX_SLOTS, DIRECTIONS), DIRECTIONS ** -0.5, 0.1875, ((0, 16), (2, 8)))
    trans_table = gaussian(seeds[7], (TRANS_TYPES, DIRECTIONS), 0.25, 1.5, ((1, 8),), jnp.float32)
    inter_list = draw_inter_list(jax.random.fold_in(seeds[12], 71), 0)
    inter_type = with_ends(jax.random.randint(seeds[9], (BOXES, LIST_LEN), 0, TRANS_TYPES), jax.random.fold_in(seeds[9], 1), 0, TRANS_TYPES - 1).astype(jnp.int32)
    near_list = with_ends(jax.random.randint(seeds[10], (BOXES, NEAR_BLOCKS), 0, BOX_GRP), jax.random.fold_in(seeds[10], 1), 0, BOX_GRP - 1).astype(jnp.int32)
    near_blocks = gaussian(seeds[11], (BOXES, NEAR_BLOCKS, BOX_SLOTS, BOX_SLOTS), BOX_SLOTS ** -0.5, 0.375, ((0, 128),))
    return dict(unknowns=unknowns, schur_blocks=schur_blocks, adjacency=adjacency, row_map=row_map, coupling=coupling, owner_box=owner_box, aggregation=aggregation, trans_table=trans_table, inter_list=inter_list, inter_type=inter_type, near_list=near_list, near_blocks=near_blocks)


def slot_ranks(owners):
    amount = owners.shape[0]
    same = owners[:, None] == owners[None, :]
    order = jnp.arange(amount, dtype=jnp.int32)
    earlier = order[:, None] > order[None, :]
    return jnp.sum(jnp.where(same & earlier, 1, 0), axis=1).astype(jnp.int32)


def reference(unknowns, schur_blocks, adjacency, row_map, coupling, owner_box, aggregation, trans_table, inter_list, inter_type, near_list, near_blocks):
    devices = N_DOM * N_DIR
    group_boxes = BOX_DEV * N_DIR
    box_total = group_boxes * N_DOM
    capacity = BOX_SLOTS // devices
    subdomains = SUB_DEV * devices
    dir_block = DIRECTIONS // N_DIR

    def schur_one(operands):
        return jnp.dot(operands[1], operands[0].T, preferred_element_type=jnp.float32)

    schur_part = lax.map(schur_one, (schur_blocks, unknowns))

    picked = unknowns[adjacency]
    row_index = jnp.broadcast_to(row_map[:, :, None, :], picked.shape)
    fetched = jnp.take_along_axis(picked, row_index, axis=3).astype(jnp.float32)
    coupled = jnp.sum(coupling[:, :, None, :] * fetched, axis=1)

    owners = owner_box[:, :, 0].reshape(devices, SUB_DEV * SURF_ROWS)
    slot_rank = lax.map(slot_ranks, owners)
    device = jnp.arange(devices, dtype=jnp.int32)[:, None]
    slot_index = ((device % N_DIR) * N_DOM + device // N_DIR) * capacity + slot_rank
    flat_index = (owners * BOX_SLOTS + slot_index).reshape(-1).astype(jnp.int32)
    surface = jnp.transpose(unknowns[:, :, :SURF_ROWS], (0, 2, 1)).reshape(-1, EXCITES)
    currents = jnp.zeros((box_total * BOX_SLOTS, EXCITES), jnp.bfloat16).at[flat_index].set(surface)
    currents = jnp.transpose(currents.reshape(box_total, BOX_SLOTS, EXCITES), (0, 2, 1))

    agg_groups = aggregation.reshape(N_DOM, group_boxes, BOX_SLOTS, DIRECTIONS)
    current_groups = currents.reshape(N_DOM, group_boxes, EXCITES, BOX_SLOTS)

    def radiate(operands):
        return jnp.einsum("hpd,hep->hed", operands[0].astype(jnp.float32), operands[1].astype(jnp.float32)).astype(jnp.bfloat16)

    patterns = lax.map(radiate, (agg_groups, current_groups)).reshape(box_total, EXCITES, DIRECTIONS)

    def respond(operands):
        listed, kinds, agg_part, nearest, blocks, group_current = operands
        sources = patterns[listed].astype(jnp.float32)
        factors = trans_table[kinds]
        incoming = jnp.einsum("hjd,hjed->hed", factors, sources).astype(jnp.bfloat16)
        agg_blocks = agg_part.astype(jnp.float32).reshape(group_boxes, BOX_SLOTS, N_DIR, dir_block)
        in_blocks = incoming.astype(jnp.float32).reshape(group_boxes, EXCITES, N_DIR, dir_block)
        far_terms = jnp.einsum("hpkd,hekd->khep", agg_blocks, in_blocks).astype(jnp.bfloat16)
        far_terms = lax.optimization_barrier(far_terms)
        far_part = jnp.sum(far_terms.astype(jnp.float32), axis=0)
        near_current = group_current[nearest].astype(jnp.float32)
        near_part = jnp.einsum("hjpq,hjeq->hep", blocks.astype(jnp.float32), near_current)
        return (far_part + near_part).astype(jnp.bfloat16)

    box_fields = lax.map(respond, (
        inter_list.reshape(N_DOM, group_boxes, LIST_LEN),
        inter_type.reshape(N_DOM, group_boxes, LIST_LEN),
        agg_groups,
        near_list.reshape(N_DOM, group_boxes, NEAR_BLOCKS),
        near_blocks.reshape(N_DOM, group_boxes, NEAR_BLOCKS, BOX_SLOTS, BOX_SLOTS),
        current_groups,
    )).reshape(box_total, EXCITES, BOX_SLOTS)

    field_table = jnp.transpose(box_fields, (0, 2, 1)).reshape(box_total * BOX_SLOTS, EXCITES)
    surface_field = field_table[flat_index].reshape(subdomains, SURF_ROWS, EXCITES)
    surface_field = jnp.transpose(surface_field, (0, 2, 1)).astype(jnp.float32)
    combined = schur_part + coupled
    return combined.at[:, :, :SURF_ROWS].add(surface_field)
```

```python
import functools

import jax
import jax.numpy as jnp
from jax import lax
from jax.experimental import pallas as pl
from jax.experimental.pallas import tpu as pltpu
from jax.sharding import PartitionSpec as P

F32 = jnp.float32
BF16 = jnp.bfloat16
I32 = jnp.int32
LANES = 128


def lane_pick(source, index):
    return jnp.take_along_axis(source, index, axis=1, mode="promise_in_bounds")


def iota(shape, axis):
    return lax.broadcasted_iota(I32, shape, axis)


def whole(shape):
    return pl.BlockSpec(shape, lambda *_: (0,) * len(shape))


SMEM_SPEC = pl.BlockSpec(memory_space=pltpu.SMEM)
ANY_SPEC = pl.BlockSpec(memory_space=pl.ANY)


def place_kernel(surface_ref, owner_ref, out_ref, spot_ref):
    blocks = owner_ref.shape[0]
    groups, copies = out_ref.shape[:2]
    box_tiles = groups // 2
    far_off = float(blocks * LANES)
    owner = owner_ref[...]
    lane = iota((LANES, LANES), 1).astype(F32)
    row = iota((LANES, LANES), 0).astype(F32)
    lowest = [None] * box_tiles
    total = [None] * box_tiles
    for t in range(blocks):
        spread = jnp.broadcast_to(owner[t : t + 1, :].astype(F32), (LANES, LANES))
        column = jnp.transpose(spread)
        number = row + (t * LANES - far_off)
        for b in range(box_tiles):
            hit = jnp.where(column == lane + float(b * LANES), number, 0.0)
            hit = hit.reshape(LANES // 8, 8, LANES)
            low = jnp.min(hit, axis=0)
            add = jnp.sum(hit, axis=0)
            lowest[b] = low if t == 0 else jnp.minimum(lowest[b], low)
            total[b] = add if t == 0 else total[b] + add
    lane8 = iota((8, LANES), 1)
    firsts = []
    seconds = []
    for b in range(box_tiles):
        low = jnp.min(lowest[b], axis=0, keepdims=True)
        add = jnp.sum(total[b], axis=0, keepdims=True)
        firsts.append(jnp.broadcast_to((low + far_off).astype(I32), (8, LANES)))
        seconds.append(jnp.broadcast_to((add - low + far_off).astype(I32), (8, LANES)))
    pieces = []
    for t in range(blocks):
        half = (t % 2) * LANES
        pieces.append(surface_ref[t // 2, :, half : half + LANES].astype(F32))
    for g in range(groups):
        b = g // 2
        if g % 2 == 0:
            source = jnp.where(lane8 < 64, firsts[b], pltpu.roll(seconds[b], 64, 1))
        else:
            source = jnp.where(lane8 < 64, pltpu.roll(firsts[b], 64, 1), seconds[b])
        within = source & (LANES - 1)
        block = source >> 7
        value = jnp.zeros((8, LANES), F32)
        for t in range(blocks):
            value = jnp.where(block == t, lane_pick(pieces[t], within), value)
        value = value.astype(BF16)
        for r in range(copies):
            out_ref[g, r] = value
    within = owner & (LANES - 1)
    box_tile = owner >> 7
    first = jnp.zeros((8, LANES), I32)
    for b in range(box_tiles):
        first = jnp.where(box_tile == b, lane_pick(firsts[b], within), first)
    own_number = iota((8, LANES), 0) * LANES + lane8
    rank = jnp.where(first == own_number, 0, 1)
    spot_ref[...] = (owner >> 6) * LANES + rank * 64 + (owner & 63)


def place(unknowns, owners, groups, copies):
    subs, excitations, _ = unknowns.shape
    surface = owners.size // subs
    return pl.pallas_call(
        place_kernel,
        grid=(1,),
        in_specs=[whole((subs, excitations, surface)), whole(owners.shape)],
        out_specs=[whole((groups, copies, excitations, LANES)), whole(owners.shape)],
        out_shape=[
            jax.ShapeDtypeStruct((groups, copies, excitations, LANES), BF16),
            jax.ShapeDtypeStruct(owners.shape, I32),
        ],
        cost_estimate=pl.CostEstimate(
            flops=8 * 1024 * 1024, bytes_accessed=300_000, transcendentals=0
        ),
        name="place",
    )(unknowns, owners)


def slot_order(count_dom, count_dir, transposed):
    size = 2 * count_dom * count_dir
    arrival = iota((size, size), 1 if transposed else 0)
    slot = iota((size, size), 0 if transposed else 1)
    source = arrival & (LANES - 1)
    shift = count_dir.bit_length() - 1
    target = ((source & (count_dir - 1)) * count_dom + (source >> shift)) * 2 + (arrival >> 7)
    return jnp.where(target == slot, 1.0, 0.0).astype(BF16)


def radiate_kernel(counts, arrived_ref, agg_ref, pattern_ref, current_ref, wide, turned):
    step = pl.program_id(0)
    boxes = pattern_ref.shape[0]
    excitations = arrived_ref.shape[1]
    half = arrived_ref.shape[2] // 2

    @pl.when(step == 0)
    def _():
        wide[...] = arrived_ref[...].astype(F32)
        for e in range(excitations):
            turned[:, e, :] = jnp.transpose(wide[:, e, :])
        first = turned[0:half].reshape(half * excitations, LANES)
        second = turned[half : 2 * half].reshape(half * excitations, LANES)
        both = jnp.concatenate([first, second], axis=1).astype(BF16)
        ordered = jnp.dot(both, slot_order(*counts, False), preferred_element_type=F32)
        current_ref[...] = ordered.astype(BF16).reshape(half, excitations, 2 * LANES)

    for n in range(boxes):
        field = lax.dot_general(
            current_ref[step * boxes + n],
            agg_ref[n],
            (((1,), (1,)), ((), ())),
            preferred_element_type=F32,
        )
        pattern_ref[n] = field.astype(BF16)


def radiate(arrived, agg, counts, step_boxes=8):
    sources, excitations, width = arrived.shape
    boxes, directions, slots = agg.shape
    return pl.pallas_call(
        functools.partial(radiate_kernel, counts),
        grid=(boxes // step_boxes,),
        in_specs=[
            whole(arrived.shape),
            pl.BlockSpec((step_boxes, directions, slots), lambda i: (i, 0, 0)),
        ],
        out_specs=[
            pl.BlockSpec((step_boxes, excitations, directions), lambda i: (i, 0, 0)),
            whole((boxes, excitations, slots)),
        ],
        out_shape=[
            jax.ShapeDtypeStruct((boxes, excitations, directions), BF16),
            jax.ShapeDtypeStruct((boxes, excitations, slots), BF16),
        ],
        scratch_shapes=[
            pltpu.VMEM((sources, excitations, width), F32),
            pltpu.VMEM((width, excitations, sources), F32),
        ],
        cost_estimate=pl.CostEstimate(
            flops=2 * boxes * 8 * directions * slots,
            bytes_accessed=2 * boxes * directions * slots,
            transcendentals=0,
        ),
        name="radiate",
    )(arrived, agg)


def near_kernel(near_ref, current_ref, block_ref, out_ref):
    step = pl.program_id(0)
    count = block_ref.shape[1]
    total = None
    for j in range(count):
        field = lax.dot_general(
            current_ref[near_ref[step * count + j]],
            block_ref[0, j],
            (((1,), (1,)), ((), ())),
            preferred_element_type=F32,
        )
        total = field if j == 0 else total + field
    out_ref[0] = total


def near(near_list, current, blocks):
    own, count, slots, _ = blocks.shape
    excitations = current.shape[1]
    return pl.pallas_call(
        near_kernel,
        grid=(own,),
        in_specs=[
            SMEM_SPEC,
            whole(current.shape),
            pl.BlockSpec((1, count, slots, slots), lambda i: (i, 0, 0, 0)),
        ],
        out_specs=pl.BlockSpec((1, excitations, slots), lambda i: (i, 0, 0)),
        out_shape=jax.ShapeDtypeStruct((own, excitations, slots), F32),
        cost_estimate=pl.CostEstimate(
            flops=2 * own * count * 8 * slots * slots,
            bytes_accessed=2 * own * count * slots * slots,
            transcendentals=0,
        ),
        name="near",
    )(near_list, current, blocks)


def couple_kernel(source_ref, before_ref, here_ref, after_ref, map_ref, coupling_ref,
                  schur_ref, out_ref, window):
    subs, links, width = map_ref.shape
    tiles = width // LANES
    window[0:subs] = before_ref[...].astype(F32)
    window[subs : 2 * subs] = here_ref[...].astype(F32)
    window[2 * subs : 3 * subs] = after_ref[...].astype(F32)
    out_ref[...] = schur_ref[...]

    def subdomain(s, carry):
        for k in range(links):
            base = source_ref[s * links + k]
            pieces = [window[base, :, q * LANES : (q + 1) * LANES] for q in range(tiles)]
            for t in range(tiles):
                cut = slice(t * LANES, (t + 1) * LANES)
                rows = jnp.broadcast_to(map_ref[s, k : k + 1, cut], (8, LANES))
                scale = jnp.broadcast_to(coupling_ref[s, k : k + 1, cut], (8, LANES))
                within = rows & (LANES - 1)
                tile = rows >> 7
                value = lane_pick(pieces[0], within)
                for q in range(1, tiles):
                    value = jnp.where(tile == q, lane_pick(pieces[q], within), value)
                out_ref[s, :, cut] += scale * value
        return carry

    lax.fori_loop(0, subs, subdomain, 0)


def couple(sources, before, here, after, row_map, coupling, schur):
    subs, excitations, width = here.shape
    same = whole(here.shape)
    return pl.pallas_call(
        couple_kernel,
        grid=(1,),
        in_specs=[SMEM_SPEC, same, same, same, whole(row_map.shape), whole(coupling.shape), same],
        out_specs=same,
        out_shape=jax.ShapeDtypeStruct(here.shape, F32),
        scratch_shapes=[pltpu.VMEM((3 * subs, excitations, width), F32)],
        cost_estimate=pl.CostEstimate(
            flops=8 * 1024 * 1024, bytes_accessed=8_000_000, transcendentals=0
        ),
        name="couple",
    )(sources, before, here, after, row_map, coupling, schur)


def receive_kernel(counts, place_ref, kind_ref, own_ref, before_ref, here_ref, after_ref,
                   table_ref, agg_ref, near_ref, out_ref, nearby, result, turned):
    step = pl.program_id(0)
    boxes, directions, slots = agg_ref.shape
    group = here_ref.shape[0]
    excitations = here_ref.shape[1]
    length = place_ref.shape[0] // group
    tail = directions - LANES

    @pl.when(step == 0)
    def _():
        nearby[0:group] = before_ref[...].astype(F32)
        nearby[group : 2 * group] = here_ref[...].astype(F32)
        nearby[2 * group : 3 * group] = after_ref[...].astype(F32)

    mine = (own_ref[0] == step).astype(F32)
    for n in range(boxes):
        head_sum = jnp.zeros((excitations, LANES), F32)
        tail_sum = jnp.zeros((excitations, tail), F32)
        for j in range(length):
            entry = (step * boxes + n) * length + j
            spot = place_ref[entry]
            kind = kind_ref[entry]
            factor = table_ref[pl.ds(kind, 1), :]
            head_sum += nearby[spot, :, 0:LANES] * factor[:, 0:LANES]
            tail_sum += nearby[spot, :, LANES:directions] * factor[:, LANES:directions]
        incoming = jnp.concatenate([head_sum, tail_sum], axis=1).astype(BF16)
        field = jnp.dot(incoming, agg_ref[n], preferred_element_type=F32)
        field = field + mine * near_ref[n]
        result[step * boxes + n] = field.astype(BF16)

    @pl.when(step == pl.num_programs(0) - 1)
    def _():
        flat = result[...].reshape(group * excitations, slots)
        ordered = jnp.dot(flat, slot_order(*counts, True), preferred_element_type=F32)
        nearby[0:group, :, 0:LANES] = ordered[:, 0:LANES].reshape(group, excitations, LANES)
        nearby[group : 2 * group, :, 0:LANES] = ordered[:, LANES:].reshape(
            group, excitations, LANES
        )
        for e in range(excitations):
            turned[:, e, :] = jnp.transpose(nearby[0 : 2 * group, e, 0:LANES])
        out_ref[...] = turned[...].astype(BF16)


def receive(places, kinds, own, before, here, after, table, agg, near_part, counts, step_boxes=8):
    boxes, directions, slots = agg.shape
    excitations = here.shape[1]
    targets = slots // 2
    same = whole(here.shape)
    return pl.pallas_call(
        functools.partial(receive_kernel, counts),
        grid=(boxes // step_boxes,),
        in_specs=[
            SMEM_SPEC,
            SMEM_SPEC,
            SMEM_SPEC,
            same,
            same,
            same,
            whole(table.shape),
            pl.BlockSpec((step_boxes, directions, slots), lambda i: (i, 0, 0)),
            whole(near_part.shape),
        ],
        out_specs=whole((targets, excitations, 2 * boxes)),
        out_shape=jax.ShapeDtypeStruct((targets, excitations, 2 * boxes), BF16),
        scratch_shapes=[
            pltpu.VMEM((3 * boxes, excitations, directions), F32),
            pltpu.VMEM((boxes, excitations, slots), BF16),
            pltpu.VMEM((targets, excitations, 2 * boxes), F32),
        ],
        cost_estimate=pl.CostEstimate(
            flops=2 * boxes * 8 * directions * slots,
            bytes_accessed=4 * boxes * directions * slots,
            transcendentals=0,
        ),
        name="receive",
    )(places, kinds, own, before, here, after, table, agg, near_part)


def finish_kernel(copies, term_ref, spot_ref, base_ref, out_ref):
    groups = term_ref.shape[0] // copies
    fields = []
    for g in range(groups):
        total = term_ref[g * copies].astype(F32)
        for k in range(1, copies):
            total = total + term_ref[g * copies + k].astype(F32)
        fields.append(total.astype(BF16).astype(F32))
    out_ref[...] = base_ref[...]
    for t in range(spot_ref.shape[0]):
        spot = jnp.broadcast_to(spot_ref[t : t + 1, :], (8, LANES))
        within = spot & (LANES - 1)
        group = spot >> 7
        value = lane_pick(fields[0], within)
        for g in range(1, groups):
            value = jnp.where(group == g, lane_pick(fields[g], within), value)
        half = (t % 2) * LANES
        out_ref[t // 2, :, half : half + LANES] += value


def finish(terms, spots, base, copies):
    return pl.pallas_call(
        functools.partial(finish_kernel, copies),
        grid=(1,),
        in_specs=[whole(terms.shape), whole(spots.shape), whole(base.shape)],
        out_specs=whole(base.shape),
        out_shape=jax.ShapeDtypeStruct(base.shape, F32),
        cost_estimate=pl.CostEstimate(
            flops=8 * 1024 * 128, bytes_accessed=600_000, transcendentals=0
        ),
        name="finish",
    )(terms, spots, base)


def both_ways(value, axis):
    count = lax.axis_size(axis)
    up = [(i, (i + 1) % count) for i in range(count)]
    down = [(j, i) for i, j in up]
    return lax.ppermute(value, axis, up), lax.ppermute(value, axis, down)


def exchange(value):
    return lax.all_to_all(value, ("dom", "dir"), split_axis=0, concat_axis=0, tiled=True)


def shards(unknowns, schur_blocks, adjacency, row_map, coupling, owner_box, aggregation,
           trans_table, inter_list, inter_type, near_list, near_blocks):
    doms = lax.axis_size("dom")
    dirs = lax.axis_size("dir")
    dom_here = lax.axis_index("dom")
    dir_here = lax.axis_index("dir")
    counts = (doms, dirs)
    subs, excitations, _ = unknowns.shape
    group = aggregation.shape[0]
    agg = jnp.swapaxes(aggregation, 1, 2)

    owners = owner_box.reshape(-1, LANES)
    placed, spots = place(unknowns, owners, doms, dirs)
    arrived = exchange(placed.reshape(doms * dirs, excitations, 2 * group))

    before_u, after_u = both_ways(unknowns, "dom")
    schur_part = jnp.einsum(
        "sij,sej->sei", schur_blocks, unknowns, preferred_element_type=F32
    )
    source_dom = adjacency // (subs * dirs)
    links = ((source_dom - dom_here + 1 + doms) % doms) * subs + adjacency % subs
    places = ((inter_list // group - dom_here + 1 + doms) % doms) * group + inter_list % group

    patterns, current = radiate(arrived, agg, counts)
    before_p, after_p = both_ways(patterns, "dom")
    near_part = near(near_list.reshape(-1), current, near_blocks)
    base = couple(links.reshape(-1), before_u, unknowns, after_u, row_map, coupling, schur_part)
    terms = receive(places.reshape(-1), inter_type.reshape(-1), dir_here.reshape(1), before_p,
                    patterns, after_p, trans_table, agg, near_part, counts)
    gathered = exchange(terms)
    return finish(gathered, spots, base, dirs)


def solution(mesh):
    split = ("dom", "dir")
    in_specs = (
        P(split, None, None),
        P(split, None, None),
        P(split, None),
        P(split, None, None),
        P(split, None, None),
        P(split, None, None),
        P("dom", None, "dir"),
        P(None, "dir"),
        P("dom", None),
        P("dom", None),
        P(split, None),
        P(split, None, None, None),
    )
    out_specs = P(split, None, None)
    return jax.shard_map(shards, mesh=mesh, in_specs=in_specs, out_specs=out_specs, check_vma=False)
```

```python
import functools

import jax
import jax.numpy as jnp
from jax import lax
from jax.experimental import pallas as pl
from jax.experimental.pallas import tpu as pltpu
from jax.sharding import PartitionSpec as P

F32 = jnp.float32
BF16 = jnp.bfloat16
I32 = jnp.int32
LANES = 128


def lane_pick(source, index):
    return jnp.take_along_axis(source, index, axis=1, mode="promise_in_bounds")


def iota(shape, axis):
    return lax.broadcasted_iota(I32, shape, axis)


SMEM_SPEC = pl.BlockSpec(memory_space=pltpu.SMEM)
VMEM_SPEC = pl.BlockSpec(memory_space=pltpu.VMEM)
HBM_SPEC = pl.BlockSpec(memory_space=pltpu.HBM)
VMEM_BYTES = 67_043_328
MIB = 1024 * 1024


def on_chip(kernel, name, spaces, operands, outputs, scratch=(), flops=0, moved=0, room=12 * MIB):
    specs = [{"s": SMEM_SPEC, "v": VMEM_SPEC, "h": HBM_SPEC}[c] for c in spaces]
    count = len(operands)
    several = isinstance(outputs, list)
    return pl.pallas_call(
        kernel,
        in_specs=specs[:count],
        out_specs=specs[count:] if several else specs[count],
        out_shape=outputs,
        scratch_shapes=list(scratch),
        compiler_params=pltpu.CompilerParams(vmem_limit_bytes=VMEM_BYTES - room),
        cost_estimate=pl.CostEstimate(flops=flops, bytes_accessed=moved, transcendentals=0),
        name=name,
    )(*operands)


def place_kernel(unknown_hbm, owner_hbm, out_hbm, spot_ref, surface_ref, owner_ref, value_ref,
                 arrive, leave):
    blocks = owner_ref.shape[0]
    groups, copies = out_hbm.shape[:2]
    owner_copy = pltpu.make_async_copy(owner_hbm, owner_ref, arrive.at[0])
    surface_copy = pltpu.make_async_copy(
        unknown_hbm.at[:, :, pl.ds(0, surface_ref.shape[2])], surface_ref, arrive.at[1]
    )
    owner_copy.start()
    surface_copy.start()
    owner_copy.wait()
    box_tiles = groups // 2
    far_off = float(blocks * LANES)
    owner = owner_ref[...]
    lane = iota((LANES, LANES), 1).astype(F32)
    row = iota((LANES, LANES), 0).astype(F32)
    lowest = [None] * box_tiles
    total = [None] * box_tiles
    for t in range(blocks):
        spread = jnp.broadcast_to(owner[t : t + 1, :].astype(F32), (LANES, LANES))
        column = jnp.transpose(spread)
        number = row + (t * LANES - far_off)
        for b in range(box_tiles):
            hit = jnp.where(column == lane + float(b * LANES), number, 0.0)
            hit = hit.reshape(LANES // 8, 8, LANES)
            low = jnp.min(hit, axis=0)
            add = jnp.sum(hit, axis=0)
            lowest[b] = low if t == 0 else jnp.minimum(lowest[b], low)
            total[b] = add if t == 0 else total[b] + add
    lane8 = iota((8, LANES), 1)
    firsts = []
    seconds = []
    for b in range(box_tiles):
        low = jnp.min(lowest[b], axis=0, keepdims=True)
        add = jnp.sum(total[b], axis=0, keepdims=True)
        firsts.append(jnp.broadcast_to((low + far_off).astype(I32), (8, LANES)))
        seconds.append(jnp.broadcast_to((add - low + far_off).astype(I32), (8, LANES)))
    surface_copy.wait()
    pieces = []
    for t in range(blocks):
        half = (t % 2) * LANES
        pieces.append(surface_ref[t // 2, :, half : half + LANES].astype(F32))
    sends = []
    for g in range(groups):
        b = g // 2
        if g % 2 == 0:
            source = jnp.where(lane8 < 64, firsts[b], pltpu.roll(seconds[b], 64, 1))
        else:
            source = jnp.where(lane8 < 64, pltpu.roll(firsts[b], 64, 1), seconds[b])
        within = source & (LANES - 1)
        block = source >> 7
        value = jnp.zeros((8, LANES), F32)
        for t in range(blocks):
            value = jnp.where(block == t, lane_pick(pieces[t], within), value)
        value_ref[g] = value.astype(BF16)
        for r in range(copies):
            if g % 4 == 3:
                part = pl.ds(g - 3, 4)
                send = pltpu.make_async_copy(
                    value_ref.at[part], out_hbm.at[part, r], leave.at[g // 4, r]
                )
                send.start()
                sends.append(send)
    within = owner & (LANES - 1)
    box_tile = owner >> 7
    first = jnp.zeros((8, LANES), I32)
    for b in range(box_tiles):
        first = jnp.where(box_tile == b, lane_pick(firsts[b], within), first)
    own_number = iota((8, LANES), 0) * LANES + lane8
    rank = jnp.where(first == own_number, 0, 1)
    spot_ref[...] = (owner >> 6) * LANES + rank * 64 + (owner & 63)
    for send in sends:
        send.wait()


def place(unknowns, owners, groups, copies):
    subs, excitations, _ = unknowns.shape
    return on_chip(
        place_kernel,
        "place",
        "hhhv",
        (unknowns, owners),
        [
            jax.ShapeDtypeStruct((groups, copies, excitations, LANES), BF16),
            jax.ShapeDtypeStruct(owners.shape, I32),
        ],
        scratch=[
            pltpu.VMEM((subs, excitations, owners.size // subs), BF16),
            pltpu.VMEM(owners.shape, I32),
            pltpu.VMEM((groups, excitations, LANES), BF16),
            pltpu.SemaphoreType.DMA((2,)),
            pltpu.SemaphoreType.DMA((groups // 4, copies)),
        ],
        flops=8 * 1024 * 1024,
        moved=300_000,
        room=0,
    )


def slot_order(count_dom, count_dir, transposed):
    size = 2 * count_dom * count_dir
    arrival = iota((size, size), 1 if transposed else 0)
    slot = iota((size, size), 0 if transposed else 1)
    source = arrival & (LANES - 1)
    shift = count_dir.bit_length() - 1
    target = ((source & (count_dir - 1)) * count_dom + (source >> shift)) * 2 + (arrival >> 7)
    return jnp.where(target == slot, 1.0, 0.0).astype(BF16)


def start_copies(source, target, done):
    count = done.shape[0]
    size = source.shape[0] // count
    copies = []
    for m in range(count):
        part = pl.ds(m * size, size)
        copies.append(pltpu.make_async_copy(source.at[part], target.at[part], done.at[m]))
        copies[m].start()
    return copies


def radiate_kernel(counts, arrived_ref, agg_hbm, pattern_ref, current_ref, wide, turned,
                   agg_ref, done):
    boxes, directions, slots = agg_ref.shape
    copies = start_copies(agg_hbm, agg_ref, done)
    excitations = arrived_ref.shape[1]
    tail = directions - LANES
    share = LANES // tail
    wide[...] = arrived_ref[...].astype(F32)
    for e in range(excitations):
        turned[:, e, :] = jnp.transpose(wide[:, e, :])
    first = turned[0:boxes].reshape(boxes * excitations, LANES)
    second = turned[boxes : 2 * boxes].reshape(boxes * excitations, LANES)
    both = jnp.concatenate([first, second], axis=1).astype(BF16)
    ordered = jnp.dot(both, slot_order(*counts, False), preferred_element_type=F32)
    current_ref[...] = ordered.astype(BF16).reshape(boxes, excitations, slots)
    for m in range(boxes // share):
        copies[m].wait()
        tails = []
        for n in range(m * share, (m + 1) * share):
            field = lax.dot_general(
                current_ref[n], agg_ref[n], (((1,), (1,)), ((), ())), preferred_element_type=F32
            )
            pattern_ref[n] = field[:, 0:LANES].astype(BF16)
            tails.append(field[:, LANES:directions])
        pattern_ref[boxes + m] = jnp.concatenate(tails, axis=1).astype(BF16)


def radiate(arrived, agg, counts):
    sources, excitations, width = arrived.shape
    boxes, directions, slots = agg.shape
    packed = boxes * directions // LANES
    return on_chip(
        functools.partial(radiate_kernel, counts),
        "radiate",
        "vhvv",
        (arrived, agg),
        [
            jax.ShapeDtypeStruct((packed, excitations, LANES), BF16),
            jax.ShapeDtypeStruct((boxes, excitations, slots), BF16),
        ],
        scratch=[
            pltpu.VMEM((sources, excitations, width), F32),
            pltpu.VMEM((width, excitations, sources), F32),
            pltpu.VMEM(agg.shape, BF16),
            pltpu.SemaphoreType.DMA((boxes // (LANES // (directions - LANES)),)),
        ],
        flops=2 * boxes * 8 * directions * slots,
        moved=2 * boxes * directions * slots,
    )


def near_kernel(near_ref, current_ref, block_hbm, out_ref, block_ref, done):
    own, count = block_ref.shape[:2]
    copies = start_copies(block_hbm, block_ref, done)
    for n in range(own):
        copies[n].wait()
        total = None
        for j in range(count):
            field = lax.dot_general(
                current_ref[near_ref[j, n]],
                block_ref[n, j],
                (((1,), (1,)), ((), ())),
                preferred_element_type=F32,
            )
            total = field if j == 0 else total + field
        out_ref[n] = total


def near(near_list, current, blocks):
    own, count, slots, _ = blocks.shape
    excitations = current.shape[1]
    return on_chip(
        near_kernel,
        "near",
        "svhv",
        (near_list, current, blocks),
        jax.ShapeDtypeStruct((own, excitations, slots), F32),
        scratch=[pltpu.VMEM(blocks.shape, BF16), pltpu.SemaphoreType.DMA((own,))],
        flops=2 * own * count * 8 * slots * slots,
        moved=2 * own * count * slots * slots,
    )


def schur_kernel(unknown_ref, schur_hbm, out_ref, schur_ref, done):
    subs = unknown_ref.shape[0]
    rows = schur_ref.shape[1]
    cuts = schur_ref.shape[0] // subs
    copies = start_copies(schur_hbm, schur_ref, done)
    for s in range(subs):
        for c in range(cuts):
            copies[s * cuts + c].wait()
            out_ref[s, :, c * rows : (c + 1) * rows] = lax.dot_general(
                unknown_ref[s],
                schur_ref[s * cuts + c],
                (((1,), (1,)), ((), ())),
                preferred_element_type=F32,
            )


def schur(unknowns, schur_blocks, cuts=2):
    subs, width, _ = schur_blocks.shape
    parts = schur_blocks.reshape(subs * cuts, width // cuts, width)
    return on_chip(
        schur_kernel,
        "schur",
        "vhv",
        (unknowns, parts),
        jax.ShapeDtypeStruct(unknowns.shape, F32),
        scratch=[pltpu.VMEM(parts.shape, BF16), pltpu.SemaphoreType.DMA((subs * cuts,))],
        flops=2 * 8 * schur_blocks.size,
        moved=2 * schur_blocks.size,
    )


def couple_kernel(source_ref, before_ref, here_ref, after_ref, map_ref, coupling_ref,
                  schur_ref, out_ref, window):
    subs, links, width = map_ref.shape
    tiles = width // LANES
    window[0:subs] = before_ref[...].astype(F32)
    window[subs : 2 * subs] = here_ref[...].astype(F32)
    window[2 * subs : 3 * subs] = after_ref[...].astype(F32)
    out_ref[...] = schur_ref[...]

    def subdomain(s, carry):
        for k in range(links):
            base = source_ref[s * links + k]
            pieces = [window[base, :, q * LANES : (q + 1) * LANES] for q in range(tiles)]
            for t in range(tiles):
                cut = slice(t * LANES, (t + 1) * LANES)
                rows = jnp.broadcast_to(map_ref[s, k : k + 1, cut], (8, LANES))
                scale = jnp.broadcast_to(coupling_ref[s, k : k + 1, cut], (8, LANES))
                within = rows & (LANES - 1)
                tile = rows >> 7
                value = lane_pick(pieces[0], within)
                for q in range(1, tiles):
                    value = jnp.where(tile == q, lane_pick(pieces[q], within), value)
                out_ref[s, :, cut] += scale * value
        return carry

    lax.fori_loop(0, subs, subdomain, 0)


def couple(sources, before, here, after, row_map, coupling, schur):
    subs, excitations, width = here.shape
    return on_chip(
        couple_kernel,
        "couple",
        "svvvvvvv",
        (sources, before, here, after, row_map, coupling, schur),
        jax.ShapeDtypeStruct(here.shape, F32),
        scratch=[pltpu.VMEM((3 * subs, excitations, width), F32)],
        flops=8 * 1024 * 1024,
        moved=8_000_000,
    )


def receive_kernel(counts, place_ref, kind_ref, own_ref, before_ref, here_ref, after_ref,
                   table_ref, agg_hbm, near_ref, out_ref, nearby, result, turned, agg_ref, done):
    boxes, directions, slots = agg_ref.shape
    copies = start_copies(agg_hbm, agg_ref, done)
    excitations = here_ref.shape[1]
    length = place_ref.shape[0]
    tail = directions - LANES
    share = LANES // tail
    own_boxes = near_ref.shape[0]

    for w, source in enumerate((before_ref, here_ref, after_ref)):
        for m in range(boxes // share):
            tails = source[boxes + m].astype(F32)
            for k in range(share):
                n = m * share + k
                row = (w * boxes + n) * 16
                nearby[row : row + 8, :] = source[n].astype(F32)
                turn = (LANES - k * tail) % LANES
                nearby[row + 8 : row + 16, :] = pltpu.roll(tails, turn, 1) if turn else tails

    for n in range(boxes):
        head_sum = None
        tail_sum = None
        for j in range(length):
            spot = pl.multiple_of(place_ref[j, n], 16)
            kind = kind_ref[j, n]
            head = nearby[pl.ds(spot, 8), :] * table_ref[pl.ds(kind, 1), :]
            rest = nearby[pl.ds(spot + 8, 8), :] * table_ref[pl.ds(kind + 1, 1), :]
            head_sum = head if j == 0 else head_sum + head
            tail_sum = rest if j == 0 else tail_sum + rest
        incoming = jnp.concatenate([head_sum, tail_sum[:, 0:tail]], axis=1).astype(BF16)
        if n % share == 0:
            copies[n // share].wait()
        field = jnp.dot(incoming, agg_ref[n], preferred_element_type=F32)
        mine = (own_ref[0] == n // own_boxes).astype(F32)
        field = field + mine * near_ref[n % own_boxes]
        result[n] = field.astype(BF16)

    flat = result[...].reshape(boxes * excitations, slots)
    ordered = jnp.dot(flat, slot_order(*counts, True), preferred_element_type=F32)
    turned[0:boxes] = ordered[:, 0:LANES].reshape(boxes, excitations, LANES)
    turned[boxes : 2 * boxes] = ordered[:, LANES:].reshape(boxes, excitations, LANES)
    pieces = [jnp.transpose(turned[:, e, :]) for e in range(excitations)]
    for e in range(excitations):
        turned[:, e, :] = pieces[e]
    out_ref[...] = turned[...].astype(BF16)


def receive(places, kinds, own, before, here, after, table, agg, near_part, counts):
    boxes, directions, slots = agg.shape
    excitations = here.shape[1]
    targets = slots // 2
    return on_chip(
        functools.partial(receive_kernel, counts),
        "receive",
        "sssvvvvhvv",
        (places, kinds, own, before, here, after, table, agg, near_part),
        jax.ShapeDtypeStruct((targets, excitations, 2 * boxes), BF16),
        scratch=[
            pltpu.VMEM((3 * boxes * 16, LANES), F32),
            pltpu.VMEM((boxes, excitations, slots), BF16),
            pltpu.VMEM((targets, excitations, 2 * boxes), F32),
            pltpu.VMEM(agg.shape, BF16),
            pltpu.SemaphoreType.DMA((boxes // (LANES // (directions - LANES)),)),
        ],
        flops=2 * boxes * 8 * directions * slots,
        moved=2 * boxes * directions * slots,
    )


def finish_kernel(copies, term_ref, spot_ref, base_ref, out_ref):
    groups = term_ref.shape[0] // copies
    fields = []
    for g in range(groups):
        total = term_ref[g * copies].astype(F32)
        for k in range(1, copies):
            total = total + term_ref[g * copies + k].astype(F32)
        fields.append(total.astype(BF16).astype(F32))
    out_ref[...] = base_ref[...]
    for t in range(spot_ref.shape[0]):
        spot = jnp.broadcast_to(spot_ref[t : t + 1, :], (8, LANES))
        within = spot & (LANES - 1)
        group = spot >> 7
        value = lane_pick(fields[0], within)
        for g in range(1, groups):
            value = jnp.where(group == g, lane_pick(fields[g], within), value)
        half = (t % 2) * LANES
        out_ref[t // 2, :, half : half + LANES] += value


def finish(terms, spots, base, copies):
    return on_chip(
        functools.partial(finish_kernel, copies),
        "finish",
        "vvvv",
        (terms, spots, base),
        jax.ShapeDtypeStruct(base.shape, F32),
        flops=8 * 1024 * 128,
        moved=600_000,
    )


def both_ways(value, axis):
    count = lax.axis_size(axis)
    up = [(i, (i + 1) % count) for i in range(count)]
    down = [(j, i) for i, j in up]
    return lax.ppermute(value, axis, up), lax.ppermute(value, axis, down)


def exchange(value):
    return lax.all_to_all(value, ("dom", "dir"), split_axis=0, concat_axis=0, tiled=True)


def shards(unknowns, schur_blocks, adjacency, row_map, coupling, owner_box, aggregation,
           trans_table, inter_list, inter_type, near_list, near_blocks):
    doms = lax.axis_size("dom")
    dirs = lax.axis_size("dir")
    dom_here = lax.axis_index("dom")
    dir_here = lax.axis_index("dir")
    counts = (doms, dirs)
    subs, excitations, _ = unknowns.shape
    group = aggregation.shape[0]
    agg = jnp.swapaxes(aggregation, 1, 2)

    owners = owner_box.reshape(-1, LANES)
    placed, spots = place(unknowns, owners, doms, dirs)
    arrived = exchange(placed.reshape(doms * dirs, excitations, 2 * group))

    before_u, after_u = both_ways(unknowns, "dom")
    schur_part = schur(unknowns, schur_blocks)
    source_dom = adjacency // (subs * dirs)
    links = ((source_dom - dom_here + 1 + doms) % doms) * subs + adjacency % subs
    listed = inter_list.T
    places = (((listed // group - dom_here + 1 + doms) % doms) * group + listed % group) * 16
    kinds = inter_type.T * 2
    table = jnp.pad(trans_table, ((0, 0), (0, 2 * LANES - trans_table.shape[1])))
    table = table.reshape(-1, LANES)
    arrived, schur_part, places, kinds, table, before_u, after_u = lax.optimization_barrier(
        (arrived, schur_part, places, kinds, table, before_u, after_u)
    )

    patterns, current = radiate(arrived, agg, counts)
    before_p, after_p = both_ways(patterns, "dom")
    near_part = near(near_list.T, current, near_blocks)
    terms = receive(places, kinds, dir_here.reshape(1), before_p, patterns, after_p,
                    table, agg, near_part, counts)
    terms, before_u, after_u = lax.optimization_barrier((terms, before_u, after_u))
    base = couple(links.reshape(-1), before_u, unknowns, after_u, row_map, coupling, schur_part)
    gathered = exchange(terms)
    return finish(gathered, spots, base, dirs)


def solution(mesh):
    split = ("dom", "dir")
    in_specs = (
        P(split, None, None),
        P(split, None, None),
        P(split, None),
        P(split, None, None),
        P(split, None, None),
        P(split, None, None),
        P("dom", None, "dir"),
        P(None, "dir"),
        P("dom", None),
        P("dom", None),
        P(split, None),
        P(split, None, None, None),
    )
    out_specs = P(split, None, None)
    return jax.shard_map(shards, mesh=mesh, in_specs=in_specs, out_specs=out_specs, check_vma=False)
```

```python
import functools

import jax
import jax.numpy as jnp
from jax import lax
from jax.experimental import pallas as pl
from jax.experimental.pallas import tpu as pltpu
from jax.sharding import PartitionSpec as P


F32 = jnp.float32
BF16 = jnp.bfloat16
I32 = jnp.int32
LANES = 128


def lane_pick(source, index):
    return jnp.take_along_axis(source, index, axis=1, mode="promise_in_bounds")


def iota(shape, axis):
    return lax.broadcasted_iota(I32, shape, axis)


SMEM_SPEC = pl.BlockSpec(memory_space=pltpu.SMEM)
VMEM_SPEC = pl.BlockSpec(memory_space=pltpu.VMEM)
HBM_SPEC = pl.BlockSpec(memory_space=pltpu.HBM)
VMEM_BYTES = 67_043_328
MIB = 1024 * 1024


def on_chip(kernel, spaces, operands, outputs, scratch=(), flops=0, moved=0, room=12 * MIB):
    specs = [{"s": SMEM_SPEC, "v": VMEM_SPEC, "h": HBM_SPEC}[c] for c in spaces]
    count = len(operands)
    several = isinstance(outputs, list)
    return pl.pallas_call(
        kernel,
        in_specs=specs[:count],
        out_specs=specs[count:] if several else specs[count],
        out_shape=outputs,
        scratch_shapes=list(scratch),
        compiler_params=pltpu.CompilerParams(vmem_limit_bytes=VMEM_BYTES - room),
        cost_estimate=pl.CostEstimate(flops=flops, bytes_accessed=moved, transcendentals=0),
    )(*operands)


def place_kernel(unknown_hbm, owner_hbm, out_hbm, spot_ref, surface_ref, owner_ref, value_ref,
                 arrive, leave):
    blocks = owner_ref.shape[0]
    groups, copies = out_hbm.shape[:2]
    owner_copy = pltpu.make_async_copy(owner_hbm, owner_ref, arrive.at[0])
    surface_copy = pltpu.make_async_copy(
        unknown_hbm.at[:, :, pl.ds(0, surface_ref.shape[2])], surface_ref, arrive.at[1]
    )
    owner_copy.start()
    surface_copy.start()
    owner_copy.wait()
    box_tiles = groups // 2
    far_off = float(blocks * LANES)
    owner = owner_ref[...]
    lane = iota((LANES, LANES), 1).astype(F32)
    row = iota((LANES, LANES), 0).astype(F32)
    lowest = [None] * box_tiles
    total = [None] * box_tiles
    for t in range(blocks):
        spread = jnp.broadcast_to(owner[t : t + 1, :].astype(F32), (LANES, LANES))
        column = jnp.transpose(spread)
        number = row + (t * LANES - far_off)
        for b in range(box_tiles):
            hit = jnp.where(column == lane + float(b * LANES), number, 0.0)
            hit = hit.reshape(LANES // 8, 8, LANES)
            low = jnp.min(hit, axis=0)
            add = jnp.sum(hit, axis=0)
            lowest[b] = low if t == 0 else jnp.minimum(lowest[b], low)
            total[b] = add if t == 0 else total[b] + add
    lane8 = iota((8, LANES), 1)
    firsts = []
    seconds = []
    for b in range(box_tiles):
        low = jnp.min(lowest[b], axis=0, keepdims=True)
        add = jnp.sum(total[b], axis=0, keepdims=True)
        firsts.append(jnp.broadcast_to((low + far_off).astype(I32), (8, LANES)))
        seconds.append(jnp.broadcast_to((add - low + far_off).astype(I32), (8, LANES)))
    surface_copy.wait()
    pieces = []
    for t in range(blocks):
        half = (t % 2) * LANES
        pieces.append(surface_ref[t // 2, :, half : half + LANES].astype(F32))
    sends = []
    for g in range(groups):
        b = g // 2
        if g % 2 == 0:
            source = jnp.where(lane8 < 64, firsts[b], pltpu.roll(seconds[b], 64, 1))
        else:
            source = jnp.where(lane8 < 64, pltpu.roll(firsts[b], 64, 1), seconds[b])
        within = source & (LANES - 1)
        block = source >> 7
        value = jnp.zeros((8, LANES), F32)
        for t in range(blocks):
            value = jnp.where(block == t, lane_pick(pieces[t], within), value)
        value_ref[g] = value.astype(BF16)
        for r in range(copies):
            if g % 4 == 3:
                part = pl.ds(g - 3, 4)
                send = pltpu.make_async_copy(
                    value_ref.at[part], out_hbm.at[part, r], leave.at[g // 4, r]
                )
                send.start()
                sends.append(send)
    within = owner & (LANES - 1)
    box_tile = owner >> 7
    first = jnp.zeros((8, LANES), I32)
    for b in range(box_tiles):
        first = jnp.where(box_tile == b, lane_pick(firsts[b], within), first)
    own_number = iota((8, LANES), 0) * LANES + lane8
    rank = jnp.where(first == own_number, 0, 1)
    spot_ref[...] = (owner >> 6) * LANES + rank * 64 + (owner & 63)
    for send in sends:
        send.wait()


def place(unknowns, owners, groups, copies):
    subs, excitations, _ = unknowns.shape
    return on_chip(
        place_kernel,
        "hhhv",
        (unknowns, owners),
        [
            jax.ShapeDtypeStruct((groups, copies, excitations, LANES), BF16),
            jax.ShapeDtypeStruct(owners.shape, I32),
        ],
        scratch=[
            pltpu.VMEM((subs, excitations, owners.size // subs), BF16),
            pltpu.VMEM(owners.shape, I32),
            pltpu.VMEM((groups, excitations, LANES), BF16),
            pltpu.SemaphoreType.DMA((2,)),
            pltpu.SemaphoreType.DMA((groups // 4, copies)),
        ],
        flops=8 * 1024 * 1024,
        moved=300_000,
        room=0,
    )


def slot_order(count_dom, count_dir, transposed):
    size = 2 * count_dom * count_dir
    arrival = iota((size, size), 1 if transposed else 0)
    slot = iota((size, size), 0 if transposed else 1)
    source = arrival & (LANES - 1)
    shift = count_dir.bit_length() - 1
    target = ((source & (count_dir - 1)) * count_dom + (source >> shift)) * 2 + (arrival >> 7)
    return jnp.where(target == slot, 1.0, 0.0).astype(BF16)


class Stream:
    def __init__(self, source, target, done, depth):
        size = source.shape[0] // done.shape[0]
        self.depth = depth
        self.copies = []
        for m in range(done.shape[0]):
            part = pl.ds(m * size, size)
            self.copies.append(
                pltpu.make_async_copy(source.at[part], target.at[part], done.at[m])
            )
        for copy in self.copies[:depth]:
            copy.start()

    def take(self, m):
        self.copies[m].wait()
        if m + self.depth < len(self.copies):
            self.copies[m + self.depth].start()


def radiate_kernel(counts, arrived_ref, agg_hbm, pattern_ref, current_ref, agg_ref, wide, turned,
                   done):
    boxes, directions, slots = agg_ref.shape
    stream = Stream(agg_hbm, agg_ref, done, 4)
    excitations = arrived_ref.shape[1]
    tail = directions - LANES
    share = LANES // tail
    wide[...] = arrived_ref[...].astype(F32)
    for e in range(excitations):
        turned[:, e, :] = jnp.transpose(wide[:, e, :])
    first = turned[0:boxes].reshape(boxes * excitations, LANES)
    second = turned[boxes : 2 * boxes].reshape(boxes * excitations, LANES)
    both = jnp.concatenate([first, second], axis=1).astype(BF16)
    ordered = jnp.dot(both, slot_order(*counts, False), preferred_element_type=F32)
    current_ref[...] = ordered.astype(BF16).reshape(boxes, excitations, slots)
    for m in range(boxes // share):
        stream.take(m)
        tails = []
        for n in range(m * share, (m + 1) * share):
            field = lax.dot_general(
                current_ref[n], agg_ref[n], (((1,), (1,)), ((), ())), preferred_element_type=F32
            )
            pattern_ref[n] = field[:, 0:LANES].astype(BF16)
            tails.append(field[:, LANES:directions])
        pattern_ref[boxes + m] = jnp.concatenate(tails, axis=1).astype(BF16)


def radiate(arrived, agg, counts):
    sources, excitations, width = arrived.shape
    boxes, directions, slots = agg.shape
    packed = boxes * directions // LANES
    return on_chip(
        functools.partial(radiate_kernel, counts),
        "vhvvv",
        (arrived, agg),
        [
            jax.ShapeDtypeStruct((packed, excitations, LANES), BF16),
            jax.ShapeDtypeStruct((boxes, excitations, slots), BF16),
            jax.ShapeDtypeStruct(agg.shape, BF16),
        ],
        scratch=[
            pltpu.VMEM((sources, excitations, width), F32),
            pltpu.VMEM((width, excitations, sources), F32),
            pltpu.SemaphoreType.DMA((boxes // (LANES // (directions - LANES)),)),
        ],
        flops=2 * boxes * 8 * directions * slots,
        moved=2 * boxes * directions * slots,
        room=16 * MIB,
    )


def near_kernel(near_ref, current_ref, block_hbm, out_ref, block_ref, done):
    own, count = block_ref.shape[:2]
    stream = Stream(block_hbm, block_ref, done, 4)
    for n in range(own):
        stream.take(n)
        total = None
        for j in range(count):
            field = lax.dot_general(
                current_ref[near_ref[j, n]],
                block_ref[n, j],
                (((1,), (1,)), ((), ())),
                preferred_element_type=F32,
            )
            total = field if j == 0 else total + field
        out_ref[n] = total


def near(near_list, current, blocks):
    own, count, slots, _ = blocks.shape
    excitations = current.shape[1]
    return on_chip(
        near_kernel,
        "svhv",
        (near_list, current, blocks),
        jax.ShapeDtypeStruct((own, excitations, slots), F32),
        scratch=[pltpu.VMEM(blocks.shape, BF16), pltpu.SemaphoreType.DMA((own,))],
        room=16 * MIB,
        flops=2 * own * count * 8 * slots * slots,
        moved=2 * own * count * slots * slots,
    )


def schur_kernel(unknown_ref, schur_hbm, out_ref, schur_ref, done):
    subs = unknown_ref.shape[0]
    rows = schur_ref.shape[1]
    cuts = schur_ref.shape[0] // subs
    stream = Stream(schur_hbm, schur_ref, done, 4)
    for s in range(subs):
        for c in range(cuts):
            stream.take(s * cuts + c)
            out_ref[s, :, c * rows : (c + 1) * rows] = lax.dot_general(
                unknown_ref[s],
                schur_ref[s * cuts + c],
                (((1,), (1,)), ((), ())),
                preferred_element_type=F32,
            )


def schur(unknowns, schur_blocks, cuts=2):
    subs, width, _ = schur_blocks.shape
    parts = schur_blocks.reshape(subs * cuts, width // cuts, width)
    return on_chip(
        schur_kernel,
        "vhv",
        (unknowns, parts),
        jax.ShapeDtypeStruct(unknowns.shape, F32),
        scratch=[pltpu.VMEM(parts.shape, BF16), pltpu.SemaphoreType.DMA((subs * cuts,))],
        flops=2 * 8 * schur_blocks.size,
        moved=2 * schur_blocks.size,
    )


def couple_kernel(source_ref, before_ref, here_ref, after_ref, map_ref, coupling_ref,
                  schur_ref, out_ref, window):
    subs, links, width = map_ref.shape
    tiles = width // LANES
    window[0:subs] = before_ref[...].astype(F32)
    window[subs : 2 * subs] = here_ref[...].astype(F32)
    window[2 * subs : 3 * subs] = after_ref[...].astype(F32)
    out_ref[...] = schur_ref[...]

    def subdomain(s, carry):
        for k in range(links):
            base = source_ref[s * links + k]
            pieces = [window[base, :, q * LANES : (q + 1) * LANES] for q in range(tiles)]
            for t in range(tiles):
                cut = slice(t * LANES, (t + 1) * LANES)
                rows = jnp.broadcast_to(map_ref[s, k : k + 1, cut], (8, LANES))
                scale = jnp.broadcast_to(coupling_ref[s, k : k + 1, cut], (8, LANES))
                within = rows & (LANES - 1)
                tile = rows >> 7
                value = lane_pick(pieces[0], within)
                for q in range(1, tiles):
                    value = jnp.where(tile == q, lane_pick(pieces[q], within), value)
                out_ref[s, :, cut] += scale * value
        return carry

    lax.fori_loop(0, subs, subdomain, 0)


def couple(sources, before, here, after, row_map, coupling, schur):
    subs, excitations, width = here.shape
    return on_chip(
        couple_kernel,
        "svvvvvvv",
        (sources, before, here, after, row_map, coupling, schur),
        jax.ShapeDtypeStruct(here.shape, F32),
        scratch=[pltpu.VMEM((3 * subs, excitations, width), F32)],
        flops=8 * 1024 * 1024,
        moved=8_000_000,
    )


def receive_kernel(counts, place_ref, kind_ref, own_ref, before_ref, here_ref, after_ref,
                   table_ref, agg_ref, near_ref, out_ref, nearby, result, turned):
    boxes, directions, slots = agg_ref.shape
    excitations = here_ref.shape[1]
    length = place_ref.shape[0]
    tail = directions - LANES
    share = LANES // tail
    own_boxes = near_ref.shape[0]

    for w, source in enumerate((before_ref, here_ref, after_ref)):
        for m in range(boxes // share):
            tails = source[boxes + m].astype(F32)
            for k in range(share):
                n = m * share + k
                row = (w * boxes + n) * 16
                nearby[row : row + 8, :] = source[n].astype(F32)
                turn = (LANES - k * tail) % LANES
                nearby[row + 8 : row + 16, :] = pltpu.roll(tails, turn, 1) if turn else tails

    for n in range(boxes):
        head_sum = None
        tail_sum = None
        for j in range(length):
            spot = pl.multiple_of(place_ref[j, n], 16)
            kind = kind_ref[j, n]
            head = nearby[pl.ds(spot, 8), :] * table_ref[pl.ds(kind, 1), :]
            rest = nearby[pl.ds(spot + 8, 8), :] * table_ref[pl.ds(kind + 1, 1), :]
            head_sum = head if j == 0 else head_sum + head
            tail_sum = rest if j == 0 else tail_sum + rest
        incoming = jnp.concatenate([head_sum, tail_sum[:, 0:tail]], axis=1).astype(BF16)
        field = jnp.dot(incoming, agg_ref[n], preferred_element_type=F32)
        mine = (own_ref[0] == n // own_boxes).astype(F32)
        result[n] = (field + mine * near_ref[n % own_boxes]).astype(BF16)

    flat = result[...].reshape(boxes * excitations, slots)
    ordered = jnp.dot(flat, slot_order(*counts, True), preferred_element_type=F32)
    turned[0:boxes] = ordered[:, 0:LANES].reshape(boxes, excitations, LANES)
    turned[boxes : 2 * boxes] = ordered[:, LANES:].reshape(boxes, excitations, LANES)
    pieces = [jnp.transpose(turned[:, e, :]) for e in range(excitations)]
    for e in range(excitations):
        turned[:, e, :] = pieces[e]
    out_ref[...] = turned[...].astype(BF16)


def receive(places, kinds, own, before, here, after, table, agg, near_part, counts):
    boxes, directions, slots = agg.shape
    excitations = here.shape[1]
    targets = slots // 2
    return on_chip(
        functools.partial(receive_kernel, counts),
        "sssvvvvvvv",
        (places, kinds, own, before, here, after, table, agg, near_part),
        jax.ShapeDtypeStruct((targets, excitations, 2 * boxes), BF16),
        scratch=[
            pltpu.VMEM((3 * boxes * 16, LANES), F32),
            pltpu.VMEM((boxes, excitations, slots), BF16),
            pltpu.VMEM((targets, excitations, 2 * boxes), F32),
        ],
        flops=2 * boxes * 8 * directions * slots,
        moved=2 * boxes * directions * slots,
        room=16 * MIB,
    )


def finish_kernel(copies, term_ref, spot_ref, base_ref, out_ref):
    groups = term_ref.shape[0] // copies
    fields = []
    for g in range(groups):
        total = term_ref[g * copies].astype(F32)
        for k in range(1, copies):
            total = total + term_ref[g * copies + k].astype(F32)
        fields.append(total.astype(BF16).astype(F32))
    out_ref[...] = base_ref[...]
    for t in range(spot_ref.shape[0]):
        spot = jnp.broadcast_to(spot_ref[t : t + 1, :], (8, LANES))
        within = spot & (LANES - 1)
        group = spot >> 7
        value = lane_pick(fields[0], within)
        for g in range(1, groups):
            value = jnp.where(group == g, lane_pick(fields[g], within), value)
        half = (t % 2) * LANES
        out_ref[t // 2, :, half : half + LANES] += value


def finish(terms, spots, base, copies):
    return on_chip(
        functools.partial(finish_kernel, copies),
        "vvvv",
        (terms, spots, base),
        jax.ShapeDtypeStruct(base.shape, F32),
        flops=8 * 1024 * 128,
        moved=600_000,
    )


def both_ways(value, axis):
    count = lax.axis_size(axis)
    up = [(i, (i + 1) % count) for i in range(count)]
    down = [(j, i) for i, j in up]
    return lax.ppermute(value, axis, up), lax.ppermute(value, axis, down)


def exchange(value):
    return lax.all_to_all(value, ("dom", "dir"), split_axis=0, concat_axis=0, tiled=True)


def shards(unknowns, schur_blocks, adjacency, row_map, coupling, owner_box, aggregation,
           trans_table, inter_list, inter_type, near_list, near_blocks):
    doms = lax.axis_size("dom")
    dirs = lax.axis_size("dir")
    dom_here = lax.axis_index("dom")
    dir_here = lax.axis_index("dir")
    counts = (doms, dirs)
    subs, excitations, _ = unknowns.shape
    group = aggregation.shape[0]
    agg = jnp.swapaxes(aggregation, 1, 2)

    owners = owner_box.reshape(-1, LANES)
    placed, spots = place(unknowns, owners, doms, dirs)
    arrived = exchange(placed.reshape(doms * dirs, excitations, 2 * group))

    before_u, after_u = both_ways(unknowns, "dom")
    source_dom = adjacency // (subs * dirs)
    links = ((source_dom - dom_here + 1 + doms) % doms) * subs + adjacency % subs
    listed = inter_list.T
    places = (((listed // group - dom_here + 1 + doms) % doms) * group + listed % group) * 16
    kinds = inter_type.T * 2
    table = jnp.pad(trans_table, ((0, 0), (0, 2 * LANES - trans_table.shape[1])))
    table = table.reshape(-1, LANES)
    dir_here = dir_here.reshape(1)
    arrived, places, kinds, table, before_u, after_u, dir_here = lax.optimization_barrier(
        (arrived, places, kinds, table, before_u, after_u, dir_here)
    )

    patterns, current, agg = radiate(arrived, agg, counts)
    before_p, after_p = both_ways(patterns, "dom")
    near_part = near(near_list.T, current, near_blocks)
    terms = receive(places, kinds, dir_here, before_p, patterns, after_p,
                    table, agg, near_part, counts)
    terms, before_u, after_u, unknowns = lax.optimization_barrier(
        (terms, before_u, after_u, unknowns)
    )
    schur_part = schur(unknowns, schur_blocks)
    base = couple(links.reshape(-1), before_u, unknowns, after_u, row_map, coupling, schur_part)
    gathered = exchange(terms)
    return finish(gathered, spots, base, dirs)


def solution(mesh):
    split = ("dom", "dir")
    in_specs = (
        P(split, None, None),
        P(split, None, None),
        P(split, None),
        P(split, None, None),
        P(split, None, None),
        P(split, None, None),
        P("dom", None, "dir"),
        P(None, "dir"),
        P("dom", None),
        P("dom", None),
        P(split, None),
        P(split, None, None, None),
    )
    out_specs = P(split, None, None)
    return jax.shard_map(shards, mesh=mesh, in_specs=in_specs, out_specs=out_specs, check_vma=False)
```

```python
import functools

import jax
import jax.numpy as jnp
from jax import lax
from jax.experimental import pallas as pl
from jax.experimental.pallas import tpu as pltpu
from jax.sharding import PartitionSpec as P


F32 = jnp.float32
BF16 = jnp.bfloat16
I32 = jnp.int32
LANES = 128


def lane_pick(source, index):
    return jnp.take_along_axis(source, index, axis=1, mode="promise_in_bounds")


def iota(shape, axis):
    return lax.broadcasted_iota(I32, shape, axis)


SMEM_SPEC = pl.BlockSpec(memory_space=pltpu.SMEM)
VMEM_SPEC = pl.BlockSpec(memory_space=pltpu.VMEM)
HBM_SPEC = pl.BlockSpec(memory_space=pltpu.HBM)
VMEM_BYTES = 67_043_328
MIB = 1024 * 1024


def on_chip(kernel, spaces, operands, outputs, scratch=(), flops=0, moved=0, room=12 * MIB):
    specs = [{"s": SMEM_SPEC, "v": VMEM_SPEC, "h": HBM_SPEC}[c] for c in spaces]
    count = len(operands)
    several = isinstance(outputs, list)
    return pl.pallas_call(
        kernel,
        in_specs=specs[:count],
        out_specs=specs[count:] if several else specs[count],
        out_shape=outputs,
        scratch_shapes=list(scratch),
        compiler_params=pltpu.CompilerParams(vmem_limit_bytes=VMEM_BYTES - room),
        cost_estimate=pl.CostEstimate(flops=flops, bytes_accessed=moved, transcendentals=0),
    )(*operands)


def place_kernel(unknown_hbm, owner_hbm, out_hbm, spot_ref, surface_ref, owner_ref, value_ref,
                 arrive, leave):
    blocks = owner_ref.shape[0]
    groups, copies = out_hbm.shape[:2]
    owner_copy = pltpu.make_async_copy(owner_hbm, owner_ref, arrive.at[0])
    surface_copy = pltpu.make_async_copy(
        unknown_hbm.at[:, :, pl.ds(0, surface_ref.shape[2])], surface_ref, arrive.at[1]
    )
    owner_copy.start()
    surface_copy.start()
    owner_copy.wait()
    box_tiles = groups // 2
    far_off = float(blocks * LANES)
    owner = owner_ref[...]
    lane = iota((LANES, LANES), 1).astype(F32)
    row = iota((LANES, LANES), 0).astype(F32)
    lowest = [None] * box_tiles
    total = [None] * box_tiles
    for t in range(blocks):
        spread = jnp.broadcast_to(owner[t : t + 1, :].astype(F32), (LANES, LANES))
        column = jnp.transpose(spread)
        number = row + (t * LANES - far_off)
        for b in range(box_tiles):
            hit = jnp.where(column == lane + float(b * LANES), number, 0.0)
            hit = hit.reshape(LANES // 8, 8, LANES)
            low = jnp.min(hit, axis=0)
            add = jnp.sum(hit, axis=0)
            lowest[b] = low if t == 0 else jnp.minimum(lowest[b], low)
            total[b] = add if t == 0 else total[b] + add
    lane8 = iota((8, LANES), 1)
    firsts = []
    seconds = []
    for b in range(box_tiles):
        low = jnp.min(lowest[b], axis=0, keepdims=True)
        add = jnp.sum(total[b], axis=0, keepdims=True)
        firsts.append(jnp.broadcast_to((low + far_off).astype(I32), (8, LANES)))
        seconds.append(jnp.broadcast_to((add - low + far_off).astype(I32), (8, LANES)))
    surface_copy.wait()
    pieces = []
    for t in range(blocks):
        half = (t % 2) * LANES
        pieces.append(surface_ref[t // 2, :, half : half + LANES].astype(F32))
    sends = []
    for g in range(groups):
        b = g // 2
        if g % 2 == 0:
            source = jnp.where(lane8 < 64, firsts[b], pltpu.roll(seconds[b], 64, 1))
        else:
            source = jnp.where(lane8 < 64, pltpu.roll(firsts[b], 64, 1), seconds[b])
        within = source & (LANES - 1)
        block = source >> 7
        value = jnp.zeros((8, LANES), F32)
        for t in range(blocks):
            value = jnp.where(block == t, lane_pick(pieces[t], within), value)
        value_ref[g] = value.astype(BF16)
        for r in range(copies):
            if g % 4 == 3:
                part = pl.ds(g - 3, 4)
                send = pltpu.make_async_copy(
                    value_ref.at[part], out_hbm.at[part, r], leave.at[g // 4, r]
                )
                send.start()
                sends.append(send)
    within = owner & (LANES - 1)
    box_tile = owner >> 7
    first = jnp.zeros((8, LANES), I32)
    for b in range(box_tiles):
        first = jnp.where(box_tile == b, lane_pick(firsts[b], within), first)
    own_number = iota((8, LANES), 0) * LANES + lane8
    rank = jnp.where(first == own_number, 0, 1)
    spot_ref[...] = (owner >> 6) * LANES + rank * 64 + (owner & 63)
    for send in sends:
        send.wait()


def place(unknowns, owners, groups, copies):
    subs, excitations, _ = unknowns.shape
    return on_chip(
        place_kernel,
        "hhhv",
        (unknowns, owners),
        [
            jax.ShapeDtypeStruct((groups, copies, excitations, LANES), BF16),
            jax.ShapeDtypeStruct(owners.shape, I32),
        ],
        scratch=[
            pltpu.VMEM((subs, excitations, owners.size // subs), BF16),
            pltpu.VMEM(owners.shape, I32),
            pltpu.VMEM((groups, excitations, LANES), BF16),
            pltpu.SemaphoreType.DMA((2,)),
            pltpu.SemaphoreType.DMA((groups // 4, copies)),
        ],
        flops=8 * 1024 * 1024,
        moved=300_000,
        room=0,
    )


def slot_order(count_dom, count_dir, transposed):
    size = 2 * count_dom * count_dir
    arrival = iota((size, size), 1 if transposed else 0)
    slot = iota((size, size), 0 if transposed else 1)
    source = arrival & (LANES - 1)
    shift = count_dir.bit_length() - 1
    target = ((source & (count_dir - 1)) * count_dom + (source >> shift)) * 2 + (arrival >> 7)
    return jnp.where(target == slot, 1.0, 0.0).astype(BF16)


class Stream:
    def __init__(self, source, target, done, depth):
        size = target.shape[0] // done.shape[0]
        skip = source.shape[0] - target.shape[0]
        self.depth = depth
        self.copies = []
        for m in range(done.shape[0]):
            taken = pl.ds(skip + m * size, size)
            part = pl.ds(m * size, size)
            self.copies.append(
                pltpu.make_async_copy(source.at[taken], target.at[part], done.at[m])
            )
        for copy in self.copies[:depth]:
            copy.start()

    def take(self, m):
        self.copies[m].wait()
        if m + self.depth < len(self.copies):
            self.copies[m + self.depth].start()


def radiate_kernel(counts, arrived_ref, early_ref, agg_hbm, pattern_ref, current_ref, agg_ref,
                   wide, turned, done):
    boxes, directions, slots = agg_hbm.shape
    early = early_ref.shape[0]
    stream = Stream(agg_hbm, agg_ref, done, 5)
    excitations = arrived_ref.shape[1]
    tail = directions - LANES
    share = LANES // tail
    wide[...] = arrived_ref[...].astype(F32)
    for e in range(excitations):
        turned[:, e, :] = jnp.transpose(wide[:, e, :])
    first = turned[0:boxes].reshape(boxes * excitations, LANES)
    second = turned[boxes : 2 * boxes].reshape(boxes * excitations, LANES)
    both = jnp.concatenate([first, second], axis=1).astype(BF16)
    ordered = jnp.dot(both, slot_order(*counts, False), preferred_element_type=F32)
    current_ref[...] = ordered.astype(BF16).reshape(boxes, excitations, slots)
    for m in range(boxes // share):
        if m * share >= early:
            stream.take(m - early // share)
        tails = []
        for n in range(m * share, (m + 1) * share):
            field = lax.dot_general(
                current_ref[n],
                early_ref[n] if n < early else agg_ref[n - early],
                (((1,), (1,)), ((), ())),
                preferred_element_type=F32,
            )
            pattern_ref[n] = field[:, 0:LANES].astype(BF16)
            tails.append(field[:, LANES:directions])
        pattern_ref[boxes + m] = jnp.concatenate(tails, axis=1).astype(BF16)


def radiate(arrived, early, agg, counts):
    sources, excitations, width = arrived.shape
    boxes, directions, slots = agg.shape
    rest = boxes - early.shape[0]
    packed = boxes * directions // LANES
    return on_chip(
        functools.partial(radiate_kernel, counts),
        "vvhvvv",
        (arrived, early, agg),
        [
            jax.ShapeDtypeStruct((packed, excitations, LANES), BF16),
            jax.ShapeDtypeStruct((boxes, excitations, slots), BF16),
            jax.ShapeDtypeStruct((rest, directions, slots), BF16),
        ],
        scratch=[
            pltpu.VMEM((sources, excitations, width), F32),
            pltpu.VMEM((width, excitations, sources), F32),
            pltpu.SemaphoreType.DMA((rest // (LANES // (directions - LANES)),)),
        ],
        flops=2 * boxes * 8 * directions * slots,
        moved=2 * boxes * directions * slots,
        room=16 * MIB,
    )


def near_kernel(near_ref, current_ref, block_ref, out_ref):
    own, count = block_ref.shape[:2]
    for n in range(own):
        total = None
        for j in range(count):
            field = lax.dot_general(
                current_ref[near_ref[j, n]],
                block_ref[n, j],
                (((1,), (1,)), ((), ())),
                preferred_element_type=F32,
            )
            total = field if j == 0 else total + field
        out_ref[n] = total


def near(near_list, current, blocks):
    own, count, slots, _ = blocks.shape
    excitations = current.shape[1]
    return on_chip(
        near_kernel,
        "svvv",
        (near_list, current, blocks),
        jax.ShapeDtypeStruct((own, excitations, slots), F32),
        room=16 * MIB,
        flops=2 * own * count * 8 * slots * slots,
        moved=2 * own * count * slots * slots,
    )


def schur_kernel(unknown_ref, schur_hbm, out_ref, schur_ref, done):
    subs = unknown_ref.shape[0]
    rows = schur_ref.shape[1]
    cuts = schur_ref.shape[0] // subs
    stream = Stream(schur_hbm, schur_ref, done, 4)
    for s in range(subs):
        for c in range(cuts):
            stream.take(s * cuts + c)
            out_ref[s, :, c * rows : (c + 1) * rows] = lax.dot_general(
                unknown_ref[s],
                schur_ref[s * cuts + c],
                (((1,), (1,)), ((), ())),
                preferred_element_type=F32,
            )


def schur(unknowns, schur_blocks, cuts=2):
    subs, width, _ = schur_blocks.shape
    parts = schur_blocks.reshape(subs * cuts, width // cuts, width)
    return on_chip(
        schur_kernel,
        "vhv",
        (unknowns, parts),
        jax.ShapeDtypeStruct(unknowns.shape, F32),
        scratch=[pltpu.VMEM(parts.shape, BF16), pltpu.SemaphoreType.DMA((subs * cuts,))],
        flops=2 * 8 * schur_blocks.size,
        moved=2 * schur_blocks.size,
    )


def couple_kernel(source_ref, before_ref, here_ref, after_ref, map_ref, coupling_ref,
                  schur_ref, out_ref, window):
    subs, links, width = map_ref.shape
    tiles = width // LANES
    window[0:subs] = before_ref[...].astype(F32)
    window[subs : 2 * subs] = here_ref[...].astype(F32)
    window[2 * subs : 3 * subs] = after_ref[...].astype(F32)
    out_ref[...] = schur_ref[...]

    def subdomain(s, carry):
        for k in range(links):
            base = source_ref[s * links + k]
            pieces = [window[base, :, q * LANES : (q + 1) * LANES] for q in range(tiles)]
            for t in range(tiles):
                cut = slice(t * LANES, (t + 1) * LANES)
                rows = jnp.broadcast_to(map_ref[s, k : k + 1, cut], (8, LANES))
                scale = jnp.broadcast_to(coupling_ref[s, k : k + 1, cut], (8, LANES))
                within = rows & (LANES - 1)
                tile = rows >> 7
                value = lane_pick(pieces[0], within)
                for q in range(1, tiles):
                    value = jnp.where(tile == q, lane_pick(pieces[q], within), value)
                out_ref[s, :, cut] += scale * value
        return carry

    lax.fori_loop(0, subs, subdomain, 0)


def couple(sources, before, here, after, row_map, coupling, schur):
    subs, excitations, width = here.shape
    return on_chip(
        couple_kernel,
        "svvvvvvv",
        (sources, before, here, after, row_map, coupling, schur),
        jax.ShapeDtypeStruct(here.shape, F32),
        scratch=[pltpu.VMEM((3 * subs, excitations, width), F32)],
        flops=8 * 1024 * 1024,
        moved=8_000_000,
    )


def receive_kernel(counts, place_ref, kind_ref, own_ref, before_ref, here_ref, after_ref,
                   table_ref, early_ref, agg_ref, near_ref, out_ref, nearby, result, turned):
    early, directions, slots = early_ref.shape
    boxes = early + agg_ref.shape[0]
    excitations = here_ref.shape[1]
    length = place_ref.shape[0]
    tail = directions - LANES
    share = LANES // tail
    own_boxes = near_ref.shape[0]

    for w, source in enumerate((before_ref, here_ref, after_ref)):
        for m in range(boxes // share):
            tails = source[boxes + m].astype(F32)
            for k in range(share):
                n = m * share + k
                row = (w * boxes + n) * 16
                nearby[row : row + 8, :] = source[n].astype(F32)
                turn = (LANES - k * tail) % LANES
                nearby[row + 8 : row + 16, :] = pltpu.roll(tails, turn, 1) if turn else tails

    for n in range(boxes):
        head_sum = None
        tail_sum = None
        for j in range(length):
            spot = pl.multiple_of(place_ref[j, n], 16)
            kind = kind_ref[j, n]
            head = nearby[pl.ds(spot, 8), :] * table_ref[pl.ds(kind, 1), :]
            rest = nearby[pl.ds(spot + 8, 8), :] * table_ref[pl.ds(kind + 1, 1), :]
            head_sum = head if j == 0 else head_sum + head
            tail_sum = rest if j == 0 else tail_sum + rest
        incoming = jnp.concatenate([head_sum, tail_sum[:, 0:tail]], axis=1).astype(BF16)
        tested = early_ref[n] if n < early else agg_ref[n - early]
        field = jnp.dot(incoming, tested, preferred_element_type=F32)
        mine = (own_ref[0] == n // own_boxes).astype(F32)
        result[n] = (field + mine * near_ref[n % own_boxes]).astype(BF16)

    flat = result[...].reshape(boxes * excitations, slots)
    ordered = jnp.dot(flat, slot_order(*counts, True), preferred_element_type=F32)
    turned[0:boxes] = ordered[:, 0:LANES].reshape(boxes, excitations, LANES)
    turned[boxes : 2 * boxes] = ordered[:, LANES:].reshape(boxes, excitations, LANES)
    pieces = [jnp.transpose(turned[:, e, :]) for e in range(excitations)]
    for e in range(excitations):
        turned[:, e, :] = pieces[e]
    out_ref[...] = turned[...].astype(BF16)


def receive(places, kinds, own, before, here, after, table, early, agg, near_part, counts):
    rest, directions, slots = agg.shape
    boxes = early.shape[0] + rest
    excitations = here.shape[1]
    targets = slots // 2
    return on_chip(
        functools.partial(receive_kernel, counts),
        "sssvvvvvvvv",
        (places, kinds, own, before, here, after, table, early, agg, near_part),
        jax.ShapeDtypeStruct((targets, excitations, 2 * boxes), BF16),
        scratch=[
            pltpu.VMEM((3 * boxes * 16, LANES), F32),
            pltpu.VMEM((boxes, excitations, slots), BF16),
            pltpu.VMEM((targets, excitations, 2 * boxes), F32),
        ],
        flops=2 * boxes * 8 * directions * slots,
        moved=2 * boxes * directions * slots,
        room=16 * MIB,
    )


def finish_kernel(copies, term_ref, spot_ref, base_ref, out_ref):
    groups = term_ref.shape[0] // copies
    fields = []
    for g in range(groups):
        total = term_ref[g * copies].astype(F32)
        for k in range(1, copies):
            total = total + term_ref[g * copies + k].astype(F32)
        fields.append(total.astype(BF16).astype(F32))
    out_ref[...] = base_ref[...]
    for t in range(spot_ref.shape[0]):
        spot = jnp.broadcast_to(spot_ref[t : t + 1, :], (8, LANES))
        within = spot & (LANES - 1)
        group = spot >> 7
        value = lane_pick(fields[0], within)
        for g in range(1, groups):
            value = jnp.where(group == g, lane_pick(fields[g], within), value)
        half = (t % 2) * LANES
        out_ref[t // 2, :, half : half + LANES] += value


def finish(terms, spots, base, copies):
    return on_chip(
        functools.partial(finish_kernel, copies),
        "vvvv",
        (terms, spots, base),
        jax.ShapeDtypeStruct(base.shape, F32),
        flops=8 * 1024 * 128,
        moved=600_000,
    )


def both_ways(value, axis):
    count = lax.axis_size(axis)
    up = [(i, (i + 1) % count) for i in range(count)]
    down = [(j, i) for i, j in up]
    return lax.ppermute(value, axis, up), lax.ppermute(value, axis, down)


def exchange(value):
    return lax.all_to_all(value, ("dom", "dir"), split_axis=0, concat_axis=0, tiled=True)


def shards(unknowns, schur_blocks, adjacency, row_map, coupling, owner_box, aggregation,
           trans_table, inter_list, inter_type, near_list, near_blocks):
    doms = lax.axis_size("dom")
    dirs = lax.axis_size("dir")
    dom_here = lax.axis_index("dom")
    dir_here = lax.axis_index("dir")
    counts = (doms, dirs)
    subs, excitations, _ = unknowns.shape
    group = aggregation.shape[0]
    agg = jnp.swapaxes(aggregation, 1, 2)

    owners = owner_box.reshape(-1, LANES)
    placed, spots = place(unknowns, owners, doms, dirs)
    arrived = exchange(placed.reshape(doms * dirs, excitations, 2 * group))

    before_u, after_u = both_ways(unknowns, "dom")
    source_dom = adjacency // (subs * dirs)
    links = ((source_dom - dom_here + 1 + doms) % doms) * subs + adjacency % subs
    listed = inter_list.T
    places = (((listed // group - dom_here + 1 + doms) % doms) * group + listed % group) * 16
    kinds = inter_type.T * 2
    table = jnp.pad(trans_table, ((0, 0), (0, 2 * LANES - trans_table.shape[1])))
    table = table.reshape(-1, LANES)
    dir_here = dir_here.reshape(1)
    early = agg[: 3 * group // 8]
    arrived, places, kinds, table, before_u, after_u, dir_here, early = lax.optimization_barrier(
        (arrived, places, kinds, table, before_u, after_u, dir_here, early)
    )

    patterns, current, agg = radiate(arrived, early, agg, counts)
    before_p, after_p = both_ways(patterns, "dom")
    near_part = near(near_list.T, current, near_blocks)
    terms = receive(places, kinds, dir_here, before_p, patterns, after_p,
                    table, early, agg, near_part, counts)
    terms, before_u, after_u, unknowns = lax.optimization_barrier(
        (terms, before_u, after_u, unknowns)
    )
    schur_part = schur(unknowns, schur_blocks)
    base = couple(links.reshape(-1), before_u, unknowns, after_u, row_map, coupling, schur_part)
    gathered = exchange(terms)
    return finish(gathered, spots, base, dirs)


def solution(mesh):
    split = ("dom", "dir")
    in_specs = (
        P(split, None, None),
        P(split, None, None),
        P(split, None),
        P(split, None, None),
        P(split, None, None),
        P(split, None, None),
        P("dom", None, "dir"),
        P(None, "dir"),
        P("dom", None),
        P("dom", None),
        P(split, None),
        P(split, None, None, None),
    )
    out_specs = P(split, None, None)
    return jax.shard_map(shards, mesh=mesh, in_specs=in_specs, out_specs=out_specs, check_vma=False)
```
